128 devices in a mesh: seq: 32 (over z, x, core), mp: 4 (over y).
Axes of the slice: x: 4, y: 4, z: 4, core: 2. Of those that a mesh axis runs over, the one named last changes fastest.
Arguments:
- grad_rows: bfloat16 [16384, 8192], P('seq', 'mp'), may hold values from -6 to 6
- img_start: int32 [256], replicated, may hold values from 0 to 16380, as said below
- img_len: int32 [256], replicated, may hold values from 4 to 64, as said below
- img_owner: int32 [256], replicated, may hold values from 0 to 31, as said below
- pre_act: bfloat16 [16384, 5120], P('seq', 'mp'), may hold values from -6 to 6
- w_out: bfloat16 [5120, 8192], P(None, 'mp'), may hold values from -0.0625 to 0.0625
Outputs:
- pre_grad: bfloat16 [16384, 5120], P('seq', 'mp')
- weight_grad: bfloat16 [5120, 8192], P('seq', 'mp')
The draws below stay inside these ranges and needn't reach their ends.
Inputs may be any that keep to these rules, and one draw needn't show every extreme that they name: Image i lies inside positions i * 64 to (i + 1) * 64 - 1: img_start[i] - i * 64 + img_len[i] <= 64. `img_len`: A multiple of 4. In every draw some owner has all its images of exactly 64 merged tokens. `img_owner`: the images i with one value of i % 8 all have different owners, and so do the 8 images of one stripe (images i with one value of i // 8).
All inputs are finite; a program needn't handle non-finite values.
Results may differ from the reference program's by a relative error of at most 0.02.
Values may be sent and summed in bfloat16 or wider, within the bound.
No kernel may reach another device: no remote copies, remote signals or barrier semaphores. Data moves between devices by JAX's collectives and lax.ppermute only.
A program may use at most 192 MiB of HBM per device.

```python
import math
import jax
import jax.numpy as jnp
from jax import lax

D_MERGE = 5120
D_OUT = 8192
STRIPE_DEV = 512
FRAME = 64
IMG_STRIPE = 8
NUM_IMG = 256
SEQ_TOT = 16384
N_SEQ = 32


def image_layout(key):
    base = jax.random.fold_in(key, 11)
    subkeys = jax.random.split(base, 4)
    stripes = NUM_IMG // IMG_STRIPE
    image_ids = jnp.arange(NUM_IMG, dtype=jnp.int32)
    lengths = 4 * jax.random.randint(subkeys[0], (NUM_IMG,), 1, FRAME // 4 + 1, dtype=jnp.int32)
    shuffle = jax.random.permutation(subkeys[1], stripes).astype(jnp.int32)
    owners = (shuffle[image_ids // IMG_STRIPE] + image_ids % IMG_STRIPE) % stripes
    chosen = jax.random.randint(subkeys[2], (), 0, stripes, dtype=jnp.int32)
    lengths = jnp.where(owners == chosen, FRAME, lengths).astype(jnp.int32)
    leftover = FRAME - lengths
    offsets = jax.random.randint(subkeys[3], (NUM_IMG,), 0, 1 << 20, dtype=jnp.int32) % (leftover + 1)
    starts = image_ids * FRAME + offsets
    return (starts.astype(jnp.int32), lengths, owners.astype(jnp.int32))


def draw_img_start(key, part):
    return image_layout(key)[0]


def draw_img_len(key, part):
    return image_layout(key)[1]


def draw_img_owner(key, part):
    return image_layout(key)[2]


def spiked(drawn, key, source, target, blocks, factor):
    def block_of(axis_at):
        return (jnp.arange(drawn.shape[axis_at]) // (drawn.shape[axis_at] // blocks)).reshape((-1,) + (1,) * (drawn.ndim - 1 - axis_at))

    one_side = jax.random.permutation(key, blocks)[block_of(target)]
    other_side = (block_of(target) + blocks // 2) % blocks
    return jnp.where((block_of(source) == one_side) | (block_of(source) == other_side), factor * drawn, drawn)


def block_scale(own_key, extent, pieces, low, top_value):
    def one(position, blocks):
        steps = jax.random.uniform(jax.random.fold_in(jax.random.fold_in(own_key, 6), position), (blocks,), jnp.float32, low / len(pieces), top_value / len(pieces))
        return jnp.repeat(jnp.exp(steps), extent[position] // blocks).reshape((-1,) + (1,) * (len(extent) - position - 1))

    level = one(*pieces[0])
    for cut in pieces[1:]:
        level = level * one(*cut)
    return level


def bell_draw(own_key, dims, deviation, limit, shards=(), kind=jnp.bfloat16):
    array = deviation * jax.random.normal(own_key, dims, jnp.float32)
    if shards:
        array = array * block_scale(own_key, dims, shards, -0.22, 0.18)
    return jnp.clip(array, -limit, limit).astype(kind)


def noise_with(key, extent, deviation, most, shards, heavy, kind=jnp.bfloat16):
    drawn = deviation * jax.random.normal(key, extent, jnp.float32)
    if shards:
        drawn = drawn * block_scale(key, extent, shards, -0.22, 0.18)
    return jnp.clip(spiked(drawn, jax.random.fold_in(key, 3), *heavy), -most, most).astype(kind)


def setup_inputs(seed: int = 0) -> dict:
    seeds = jax.random.split(jax.random.key(seed), 7)
    grad_rows = bell_draw(seeds[0], (SEQ_TOT, D_OUT), 1.0, 6.0, ((0, 32), (1, 4)))
    img_start = draw_img_start(jax.random.fold_in(seeds[6], 71), 0)
    img_len = draw_img_len(jax.random.fold_in(seeds[6], 71), 0)
    img_owner = draw_img_owner(jax.random.fold_in(seeds[6], 71), 0)
    pre_act = noise_with(seeds[4], (SEQ_TOT, D_MERGE), 1.0, 6.0, ((0, 32), (1, 4)), (0, 1, 32, 2.75))
    w_out = bell_draw(seeds[5], (D_MERGE, D_OUT), D_OUT ** -0.5, 0.0625, ((1, 4),))
    return dict(grad_rows=grad_rows, img_start=img_start, img_len=img_len, img_owner=img_owner, pre_act=pre_act, w_out=w_out)


def gelu_parts(values):
    normal_cdf = 0.5 * (1.0 + lax.erf(values * 0.7071067811865476))
    density = jnp.exp(-0.5 * values * values) * 0.3989422804014327
    return (values * normal_cdf, normal_cdf + values * density)

def reference(grad_rows, img_start, img_len, img_owner, pre_act, w_out):
    frames = STRIPE_DEV // FRAME
    image_ids = jnp.arange(NUM_IMG, dtype=jnp.int32)
    within = jnp.arange(FRAME, dtype=jnp.int32)
    slot_ids = (img_owner * STRIPE_DEV + image_ids % frames * FRAME)[:, None] + within[None, :]
    positions = jnp.clip(img_start[:, None] + within[None, :], 0, SEQ_TOT - 1).astype(jnp.int32)
    filled = within[None, :] < img_len[:, None]
    picked = jnp.where(filled[:, :, None], grad_rows[positions], jnp.zeros((), jnp.bfloat16))
    routed = jnp.zeros((SEQ_TOT, D_OUT), jnp.bfloat16).at[slot_ids.reshape(-1)].set(picked.reshape(-1, D_OUT))
    hidden_grad = lax.dot_general(routed, w_out, (((1,), (1,)), ((), ())), preferred_element_type=jnp.float32)
    activation, derivative = gelu_parts(pre_act.astype(jnp.float32))
    activation = activation.astype(jnp.bfloat16)
    pre_grad = (hidden_grad * derivative).astype(jnp.bfloat16)
    factor = 1.0 / math.sqrt(SEQ_TOT)

    def accumulate(running, owner_block):
        owner_act, owner_rows = owner_block
        partial_value = lax.dot_general(owner_act, owner_rows, (((0,), (0,)), ((), ())), preferred_element_type=jnp.float32) * factor
        partial_value = lax.optimization_barrier(partial_value.astype(jnp.bfloat16))
        return (running + partial_value.astype(jnp.float32), None)
    weight_grad, _ = lax.scan(accumulate, jnp.zeros((D_MERGE, D_OUT), jnp.float32), (activation.reshape(N_SEQ, STRIPE_DEV, D_MERGE), routed.reshape(N_SEQ, STRIPE_DEV, D_OUT)))
    return (pre_grad, weight_grad.astype(jnp.bfloat16))
```

```python
import math

import jax
import jax.numpy as jnp
from jax import lax
from jax.experimental import pallas as pl
from jax.experimental.pallas import tpu as pltpu
from jax.sharding import Mesh
from jax.sharding import PartitionSpec as P

FRAME = 64
SEQ = ("z", "x", "core")


def flip(value, axis, mask):
    size = lax.axis_size(axis)
    return lax.ppermute(value, axis, [(i, i ^ mask) for i in range(size)])


def gelu_parts(values):
    normal_cdf = 0.5 * (1.0 + lax.erf(values * 0.7071067811865476))
    density = jnp.exp(-0.5 * values * values) * 0.3989422804014327
    return (values * normal_cdf, normal_cdf + values * density)


def place_kernel(owner_ref, blocks_ref, out_ref, staged, sem):
    def move(i, carry):
        staged[owner_ref[i]] = blocks_ref[i]
        return carry

    lax.fori_loop(0, blocks_ref.shape[0], move, 0)
    copy = pltpu.make_async_copy(staged, out_ref, sem)
    copy.start()
    copy.wait()


def place(owner, blocks):
    return pl.pallas_call(
        place_kernel,
        out_shape=jax.ShapeDtypeStruct(blocks.shape, blocks.dtype),
        in_specs=[pl.BlockSpec(memory_space=pltpu.SMEM), pl.BlockSpec(memory_space=pltpu.VMEM)],
        out_specs=pl.BlockSpec(memory_space=pltpu.HBM),
        scratch_shapes=[pltpu.VMEM(blocks.shape, blocks.dtype), pltpu.SemaphoreType.DMA],
        compiler_params=pltpu.CompilerParams(vmem_limit_bytes=12 << 20),
        cost_estimate=pl.CostEstimate(
            flops=0, transcendentals=0, bytes_accessed=2 * blocks.size * blocks.dtype.itemsize
        ),
    )(owner, blocks)


def hidden_kernel(rows_ref, weights_ref, out_ref):
    terms = dot(rows_ref[...], weights_ref[...], ((1,), (1,)))
    out_ref[0] = terms.astype(out_ref.dtype)


def hidden_terms(rows, weights, first, count, width):
    tokens, depth = rows.shape
    per_device = weights.shape[0] // 4 // width
    return pl.pallas_call(
        hidden_kernel,
        grid=(4, count),
        out_shape=jax.ShapeDtypeStruct((4, tokens, count * width), jnp.bfloat16),
        in_specs=[
            pl.BlockSpec((tokens, depth), lambda d, j: (0, 0)),
            pl.BlockSpec((width, depth), lambda d, j: (d * per_device + first + j, 0)),
        ],
        out_specs=pl.BlockSpec((1, tokens, width), lambda d, j: (d, 0, j)),
        compiler_params=pltpu.CompilerParams(vmem_limit_bytes=16 << 20),
        cost_estimate=pl.CostEstimate(
            flops=8 * tokens * depth * count * width,
            transcendentals=0,
            bytes_accessed=2 * (tokens * depth + 4 * count * width * (depth + tokens)),
        ),
    )(rows, pltpu.with_memory_space_constraint(weights, pltpu.HBM))


def dot(lhs, rhs, dims):
    return lax.dot_general(lhs, rhs, (dims, ((), ())), preferred_element_type=jnp.float32)


def wide(value):
    return value.astype(jnp.float32)


def narrow(value):
    return value.astype(jnp.bfloat16)


def take(value, masks, axis):
    parts = [lax.dynamic_slice_in_dim(value, m, 1, axis) for m in masks]
    return jnp.concatenate(parts, axis)


def after(value, *others):
    return lax.optimization_barrier((value, *others))[0]


def gather_ring(value, gate):
    half = value.shape[0] // 2
    one, three = after((flip(value, "y", 1), flip(value, "y", 3)), gate)
    two = jnp.concatenate([flip(one[:half], "y", 3), flip(three[half:], "y", 1)], axis=0)
    return jnp.stack([value, one, two, three])


def product(part, rhs):
    return narrow(dot(part, rhs, ((1,), (0,)))).reshape(2, 4, -1, rhs.shape[1])


SENT = {1: slice(1, 3), 3: slice(2, 4)}
HELD = {1: slice(3, 5), 3: slice(0, 2)}
OWN, FAR = {1: 1, 3: 0}, {1: 0, 3: 1}
OWN_SENT, FAR_SENT = {1: 0, 3: 1}, {1: 1, 3: 0}


def scatter_first(arrived, kept, axis, near):
    far = 4 - near
    arrived_far = flip(narrow(wide(kept[FAR[near]]) + wide(arrived[FAR_SENT[near]])), axis, far)
    return narrow(wide(kept[OWN[near]]) + wide(arrived[OWN_SENT[near]]) + wide(arrived_far))


def scatter_second(total, axis, near):
    far = 4 - near
    arrived = flip(total[SENT[near]], axis, near)
    arrived_far = flip(narrow(wide(total[far]) + wide(arrived[FAR_SENT[near]])), axis, far)
    return wide(total[0]) + wide(arrived[OWN_SENT[near]]) + wide(arrived_far)


def local(grad_rows, img_start, img_len, img_owner, pre_act, w_out):
    stripe, quarter = grad_rows.shape
    owners_total = lax.axis_size(SEQ)
    frames = stripe // FRAME
    here = lax.axis_index(SEQ)
    x, y, z, core = (lax.axis_index(a) for a in ("x", "y", "z", "core"))
    piece = stripe // owners_total

    spread = lax.all_to_all(
        grad_rows.reshape(owners_total, piece, quarter), SEQ, split_axis=0, concat_axis=0, tiled=True
    )
    owners = img_owner.reshape(owners_total, frames)
    frame_here = here * piece // FRAME
    owner_here = lax.dynamic_index_in_dim(owners, frame_here, 1, keepdims=False)
    placed = place(owner_here, spread)
    rows = lax.all_to_all(placed, SEQ, split_axis=0, concat_axis=0, tiled=True).reshape(stripe, quarter)

    mine = (owners == here).astype(jnp.int32)
    image_ids = jnp.arange(owners_total * frames, dtype=jnp.int32)
    offsets = (mine * (img_start - image_ids * FRAME).reshape(owners_total, frames)).sum(axis=0)
    lengths = (mine * img_len.reshape(owners_total, frames)).sum(axis=0)
    within = jnp.arange(FRAME, dtype=jnp.int32)
    target = jnp.arange(frames, dtype=jnp.int32)[:, None] * FRAME + offsets[:, None] + within[None, :]
    target = jnp.where(within[None, :] < lengths[:, None], target, -1).reshape(1, stripe)
    chosen = (target == jnp.arange(stripe, dtype=jnp.int32)[:, None]).astype(jnp.bfloat16)

    units = pre_act.shape[1]
    _, derivative = gelu_parts(dot(chosen, pre_act, ((1,), (0,))))
    activation, _ = gelu_parts(dot(pre_act, chosen, ((0,), (1,))))
    halves = take(narrow(activation).reshape(4, 2, units // 8, stripe), [x ^ m for m in range(4)], 0)
    own_half = lax.dynamic_index_in_dim(halves, core, 1, keepdims=False)
    other_half = flip(lax.dynamic_index_in_dim(halves, 1 - core, 1, keepdims=False), "core", 1)
    both = jnp.concatenate([own_half, other_half], axis=2)
    by_z = take(gather_ring(both, placed), [y ^ z ^ m for m in (0, 1, 2, 3, 0)], 0)
    by_x = jnp.swapaxes(by_z[:4], 0, 1)
    by_x = jnp.concatenate([by_x, by_x[:1]], axis=0)
    source = {"x": by_x, "z": by_z}

    lhs = {}
    for axis, near in (("x", 1), ("z", 1), ("x", 3), ("z", 3)):
        depth = 2 * stripe
        lhs[axis, near] = [source[axis][part[near]].reshape(-1, depth) for part in (SENT, HELD)]
    rows, weights, lhs = lax.optimization_barrier((rows, w_out, lhs))

    width = units // 5

    def hidden_rest(terms, gate, start, stop):
        arrived = after(lax.all_to_all(terms, "y", split_axis=0, concat_axis=0, tiled=True), gate)
        grad = narrow(wide(arrived).sum(axis=0) * derivative[:, start:stop])
        return narrow(dot(chosen, grad, ((0,), (0,))))

    early = hidden_terms(rows, weights, 0, 1, width)

    pair = jnp.concatenate([rows, flip(rows, "core", 1)], axis=0)
    span = quarter // 4
    plans = (("x", "z", 1), ("z", "x", 1), ("x", "z", 3), ("z", "x", 3))
    columns = [pair[:, i * span : (i + 1) * span] for i in range(4)]
    terms = [product(lhs[first, near][0], c) for (first, _, near), c in zip(plans, columns)]
    landed = [flip(term, first, near) for (first, _, near), term in zip(plans, terms)]

    late = hidden_terms(rows, after(weights, *terms), 1, 4, width)
    lhs = after(lhs, late)
    kept = [product(lhs[first, near][1], c) for (first, _, near), c in zip(plans, columns)]

    totals = [scatter_first(a, k, first, near) for a, k, (first, _, near) in zip(landed, kept, plans)]
    sums = [scatter_second(t, second, near) for t, (_, second, near) in zip(totals, plans)]
    factor = 1.0 / math.sqrt(owners_total * stripe)
    weight_grad = narrow(jnp.concatenate(sums, axis=1) * factor)
    parts = [hidden_rest(early, kept[0], 0, width), hidden_rest(late, kept[0], width, units)]
    pre_grad = jnp.concatenate(parts, axis=1)
    return (pre_grad, weight_grad)


def solution(mesh):
    grid = Mesh(mesh.devices.reshape(4, 4, 2, 4), ("z", "x", "core", "y"))
    return jax.shard_map(
        local,
        mesh=grid,
        in_specs=(P(SEQ, "y"), P(), P(), P(), P(SEQ, "y"), P(None, "y")),
        out_specs=(P(SEQ, "y"), P(SEQ, "y")),
        check_vma=False,
    )
```

```python
import functools
import math

import jax
import jax.numpy as jnp
from jax import lax
from jax.experimental import pallas as pl
from jax.experimental.pallas import tpu as pltpu
from jax.sharding import Mesh
from jax.sharding import PartitionSpec as P

FRAME = 64
SEQ = ("z", "x", "core")


def flip(value, axis, mask):
    size = lax.axis_size(axis)
    return lax.ppermute(value, axis, [(i, i ^ mask) for i in range(size)])


def gelu_parts(values):
    normal_cdf = 0.5 * (1.0 + lax.erf(values * 0.7071067811865476))
    density = jnp.exp(-0.5 * values * values) * 0.3989422804014327
    return (values * normal_cdf, normal_cdf + values * density)


def place_kernel(owner_ref, blocks_ref, out_ref, staged, sem):
    def move(i, carry):
        staged[owner_ref[i]] = blocks_ref[i]
        return carry

    lax.fori_loop(0, blocks_ref.shape[0], move, 0)
    copy = pltpu.make_async_copy(staged, out_ref, sem)
    copy.start()
    copy.wait()


def place(owner, blocks):
    return pl.pallas_call(
        place_kernel,
        out_shape=pltpu.HBM(blocks.shape, blocks.dtype),
        in_specs=[pl.BlockSpec(memory_space=pltpu.SMEM), pl.BlockSpec(memory_space=pltpu.VMEM)],
        out_specs=pl.BlockSpec(memory_space=pltpu.HBM),
        scratch_shapes=[pltpu.VMEM(blocks.shape, blocks.dtype), pltpu.SemaphoreType.DMA],
        compiler_params=pltpu.CompilerParams(vmem_limit_bytes=12 << 20),
        cost_estimate=pl.CostEstimate(
            flops=0, transcendentals=0, bytes_accessed=2 * blocks.size * blocks.dtype.itemsize
        ),
    )(owner, blocks)


def hidden_kernel(rows_ref, weights_ref, out_ref):
    part = weights_ref[...].reshape(-1, weights_ref.shape[-1])
    out_ref[0] = dot(rows_ref[...], part, ((1,), (1,))).astype(out_ref.dtype)


def hidden_terms(rows, weights, first, count):
    tokens, depth = rows.shape
    width = weights.shape[2]
    return pl.pallas_call(
        hidden_kernel,
        grid=(4,),
        out_shape=pltpu.HBM((4, tokens, count * width), jnp.bfloat16),
        in_specs=[
            pl.BlockSpec((tokens, depth), lambda d: (0, 0)),
            pl.BlockSpec((1, count, width, depth), lambda d: (d, first // count, 0, 0)),
        ],
        out_specs=pl.BlockSpec((1, tokens, count * width), lambda d: (d, 0, 0)),
        compiler_params=pltpu.CompilerParams(vmem_limit_bytes=18 << 20),
        cost_estimate=pl.CostEstimate(
            flops=8 * tokens * depth * count * width,
            transcendentals=0,
            bytes_accessed=2 * (tokens * depth + 4 * count * width * (depth + tokens)),
        ),
    )(rows, pltpu.with_memory_space_constraint(weights, pltpu.HBM))


def dot(lhs, rhs, dims):
    return lax.dot_general(lhs, rhs, (dims, ((), ())), preferred_element_type=jnp.float32)


def wide(value):
    return value.astype(jnp.float32)


def narrow(value):
    return value.astype(jnp.bfloat16)


def after(value, *others):
    return lax.optimization_barrier((value, *others))[0]


def gather_ring(value, other):
    half = value.shape[0] // 2
    low, high = value[:half], value[half:]
    first = flip(low, "y", 1), flip(high, "y", 3)
    low, high, one_low, three_high, other = lax.optimization_barrier((low, high, *first, other))
    two_low, two_high = flip(one_low, "y", 3), flip(three_high, "y", 1)
    return [value, one_low, flip(high, "y", 1), flip(low, "y", 3), three_high, two_low, two_high], other


PLANS = (("x", "z", 1), ("z", "x", 1), ("x", "z", 3), ("z", "x", 3))


def arrange_kernel(starts, order_ref, *refs):
    inputs, outputs = refs[: len(starts)], refs[-len(PLANS) :]
    step = pl.program_id(0)
    for k, start in enumerate(starts):
        stop = starts[k + 1] if k + 1 < len(starts) else 16

        @pl.when((step >= start) & (step < stop))
        def _(k=k):
            for out_ref in outputs:
                out_ref[...] = inputs[k][...]


def arrange(pieces, order, offset, before=()):
    starts, total = [], 0
    for piece in pieces:
        starts.append(total)
        total += piece.shape[0]
    block = (1, *pieces[0].shape[1:])

    def source(start, count):
        return lambda i, order: (jnp.clip(i - start, 0, count - 1), 0, 0)

    def target(first, near):
        lead = 3 if near == 1 else 2

        def index(i, order):
            place = lax.shift_right_logical(i + offset, 2)
            z, x = place ^ lax.shift_right_logical(place, 1) ^ order[0], i & 3
            major, minor = (x, z) if first == "x" else (z, x)
            return (((major + lead) & 3) * 4 + minor, 0, 0)

        return index

    size = total * block[1] * block[2] * 2
    return pl.pallas_call(
        functools.partial(arrange_kernel, starts),
        grid_spec=pltpu.PrefetchScalarGridSpec(
            num_scalar_prefetch=1,
            grid=(total,),
            in_specs=[pl.BlockSpec(block, source(s, p.shape[0])) for s, p in zip(starts, pieces)]
            + [pl.BlockSpec(memory_space=pltpu.HBM) for _ in before],
            out_specs=[pl.BlockSpec(block, target(first, near)) for first, _, near in PLANS],
        ),
        out_shape=[pltpu.HBM((16, *block[1:]), jnp.bfloat16) for _ in PLANS],
        input_output_aliases={1 + len(pieces) + i: i for i in range(len(before))},
        compiler_params=pltpu.CompilerParams(vmem_limit_bytes=8 << 20),
        cost_estimate=pl.CostEstimate(flops=0, transcendentals=0, bytes_accessed=5 * size),
    )(order, *pieces, *before)


def product(part, rhs):
    return narrow(dot(part, rhs, ((1,), (0,)))).reshape(2, 4, -1, rhs.shape[1])


SENT = {1: slice(1, 3), 3: slice(2, 4)}
HELD = {1: slice(3, 5), 3: slice(0, 2)}
OWN, FAR = {1: 1, 3: 0}, {1: 0, 3: 1}
OWN_SENT, FAR_SENT = {1: 0, 3: 1}, {1: 1, 3: 0}


def scatter_first(arrived, kept, axis, near):
    far = 4 - near
    arrived_far = flip(narrow(wide(kept[FAR[near]]) + wide(arrived[FAR_SENT[near]])), axis, far)
    return narrow(wide(kept[OWN[near]]) + wide(arrived[OWN_SENT[near]]) + wide(arrived_far))


def scatter_second(total, axis, near):
    far = 4 - near
    arrived = flip(total[SENT[near]], axis, near)
    arrived_far = flip(narrow(wide(total[far]) + wide(arrived[FAR_SENT[near]])), axis, far)
    return wide(total[0]) + wide(arrived[OWN_SENT[near]]) + wide(arrived_far)


def local(grad_rows, img_start, img_len, img_owner, pre_act, w_out):
    stripe, quarter = grad_rows.shape
    owners_total = lax.axis_size(SEQ)
    frames = stripe // FRAME
    here = lax.axis_index(SEQ)
    x, y, z, core = (lax.axis_index(a) for a in ("x", "y", "z", "core"))
    piece = stripe // owners_total

    spread = lax.all_to_all(
        grad_rows.reshape(owners_total, piece, quarter), SEQ, split_axis=0, concat_axis=0, tiled=True
    )

    images = owners_total * frames
    image_ids = jnp.arange(images, dtype=jnp.int32)
    slots = jnp.arange(stripe, dtype=jnp.int32)
    chosen_image = (image_ids % frames == (slots // FRAME)[:, None]) & (img_owner == here)
    packed = (img_start - image_ids * FRAME) * (2 * FRAME) + img_len
    packed = jnp.where(chosen_image, packed, 0).sum(axis=1)
    offset, length = packed // (2 * FRAME), packed % (2 * FRAME)
    target = jnp.where(slots % FRAME < length, slots + offset, -1)
    chosen = (target[:, None] == slots).astype(jnp.bfloat16)

    units = pre_act.shape[1]
    _, derivative = gelu_parts(dot(chosen, pre_act, ((0,), (0,))))
    activation, _ = gelu_parts(dot(pre_act, chosen, ((0,), (0,))))
    halves = narrow(activation).reshape(4, 2, units // 8, stripe)

    def half_of(which):
        shape = (1, 1, *halves.shape[2:])
        parts = [lax.dynamic_slice(halves, (x ^ m, which, 0, 0), shape)[:, 0] for m in range(4)]
        return jnp.concatenate(parts, axis=0)

    both = jnp.concatenate([half_of(core), flip(half_of(1 - core), "core", 1)], axis=2)
    pieces, spread = gather_ring(both, spread)
    order = (y ^ z).reshape(1)
    arranged = arrange(pieces[5:], order, 12, arrange(pieces[:5], order, 0))
    owners = img_owner.reshape(owners_total, frames)
    frame_here = here * piece // FRAME
    owner_here = lax.dynamic_index_in_dim(owners, frame_here, 1, keepdims=False)
    placed = place(owner_here, spread)
    rows = lax.all_to_all(placed, SEQ, split_axis=0, concat_axis=0, tiled=True).reshape(stripe, quarter)
    lhs = [part.reshape(-1, 2 * stripe) for part in arranged]
    weights = w_out.reshape(4, 5, units // 5, quarter)
    rows, weights, lhs, derivative = lax.optimization_barrier((rows, weights, lhs, derivative))

    cut = units * 4 // 5

    def exchange(terms):
        return lax.all_to_all(terms, "y", split_axis=0, concat_axis=0, tiled=True)

    def hidden_rest(arrived, start, stop):
        grad = narrow(wide(arrived).sum(axis=0) * derivative[:, start:stop])
        return narrow(dot(chosen, grad, ((1,), (0,))))

    early = hidden_terms(rows, weights, 4, 1)

    pair = jnp.concatenate([rows, flip(rows, "core", 1)], axis=0)
    span = quarter // 4
    columns = [pair[:, i * span : (i + 1) * span] for i in range(4)]
    terms = [product(part[: part.shape[0] // 2], c) for part, c in zip(lhs, columns)]
    landed = [flip(term, first, near) for (first, _, near), term in zip(PLANS, terms)]

    done = [term[0, 0, :8, :128] for term in terms]
    early = exchange(after(early, *done))
    late = hidden_terms(rows, after(weights, *done), 0, 4)
    lhs, early, _ = lax.optimization_barrier((lhs, early, late))
    late = exchange(late)
    kept = [product(part[part.shape[0] // 2 :], c) for part, c in zip(lhs, columns)]

    totals = [scatter_first(a, k, first, near) for a, k, (first, _, near) in zip(landed, kept, PLANS)]
    sums = [scatter_second(t, second, near) for t, (_, second, near) in zip(totals, PLANS)]
    factor = 1.0 / math.sqrt(owners_total * stripe)
    weight_grad = narrow(jnp.concatenate(sums, axis=1) * factor)
    parts = [hidden_rest(late, 0, cut), hidden_rest(early, cut, units)]
    pre_grad = jnp.concatenate(parts, axis=1)
    return (pre_grad, weight_grad)


def solution(mesh):
    grid = Mesh(mesh.devices.reshape(4, 4, 2, 4), ("z", "x", "core", "y"))
    return jax.shard_map(
        local,
        mesh=grid,
        in_specs=(P(SEQ, "y"), P(), P(), P(), P(SEQ, "y"), P(None, "y")),
        out_specs=(P(SEQ, "y"), P(SEQ, "y")),
        check_vma=False,
    )
```

```python
import functools
import math

import jax
import jax.numpy as jnp
from jax import lax
from jax.experimental import pallas as pl
from jax.experimental.pallas import tpu as pltpu
from jax.sharding import Mesh
from jax.sharding import PartitionSpec as P

FRAME = 64
SEQ = ("z", "x", "core")


def flip(value, axis, mask):
    size = lax.axis_size(axis)
    return lax.ppermute(value, axis, [(i, i ^ mask) for i in range(size)])


def gelu_parts(values):
    normal_cdf = 0.5 * (1.0 + lax.erf(values * 0.7071067811865476))
    density = jnp.exp(-0.5 * values * values) * 0.3989422804014327
    return (values * normal_cdf, normal_cdf + values * density)


def place_kernel(owner_ref, blocks_ref, out_ref, staged, in_sems, out_sems):
    count = blocks_ref.shape[0]

    def read(i):
        return pltpu.make_async_copy(blocks_ref.at[i], staged.at[i], in_sems.at[i])

    def write(i):
        return pltpu.make_async_copy(staged.at[i], out_ref.at[owner_ref[i]], out_sems.at[i])

    def start(i, carry):
        read(i).start()
        return carry

    def move(i, carry):
        read(i).wait()
        write(i).start()
        return carry

    def wait(i, carry):
        write(i).wait()
        return carry

    for step in (start, move, wait):
        lax.fori_loop(0, count, step, 0)


def place(owner, blocks):
    return pl.pallas_call(
        place_kernel,
        out_shape=pltpu.HBM(blocks.shape, blocks.dtype),
        in_specs=[pl.BlockSpec(memory_space=pltpu.SMEM), pl.BlockSpec(memory_space=pltpu.HBM)],
        out_specs=pl.BlockSpec(memory_space=pltpu.HBM),
        scratch_shapes=[
            pltpu.VMEM(blocks.shape, blocks.dtype),
            pltpu.SemaphoreType.DMA((blocks.shape[0],)),
            pltpu.SemaphoreType.DMA((blocks.shape[0],)),
        ],
        compiler_params=pltpu.CompilerParams(vmem_limit_bytes=8 << 20),
        cost_estimate=pl.CostEstimate(
            flops=0, transcendentals=0, bytes_accessed=2 * blocks.size * blocks.dtype.itemsize
        ),
    )(owner, blocks)


def finish_kernel(target_ref, late_ref, early_ref, derivative_ref, out_ref, chosen):
    step = pl.program_id(0)

    @pl.when(step == 0)
    def _():
        rows = lax.broadcasted_iota(jnp.int32, chosen.shape, 1)
        chosen[...] = jnp.where(rows == target_ref[...], 1.0, 0.0).astype(jnp.bfloat16)

    def put(arrived):
        total = wide(arrived[0]) + wide(arrived[1]) + wide(arrived[2]) + wide(arrived[3])
        grad = narrow(total * derivative_ref[...])
        out_ref[...] = narrow(dot(chosen[...], grad, ((1,), (0,))))

    last = pl.num_programs(0) - 1

    @pl.when(step < last)
    def _():
        put(late_ref[...])

    @pl.when(step == last)
    def _():
        put(early_ref[...])


def finish(target, late, early, derivative):
    tokens, width = early.shape[1:]
    count = late.shape[2] // width
    return pl.pallas_call(
        finish_kernel,
        grid=(count + 1,),
        out_shape=jax.ShapeDtypeStruct(derivative.shape, jnp.bfloat16),
        in_specs=[
            pl.BlockSpec((tokens, 1), lambda j: (0, 0)),
            pl.BlockSpec((4, tokens, width), lambda j: (0, 0, jnp.minimum(j, count - 1))),
            pl.BlockSpec((4, tokens, width), lambda j: (0, 0, 0)),
            pl.BlockSpec((tokens, width), lambda j: (0, j)),
        ],
        out_specs=pl.BlockSpec((tokens, width), lambda j: (0, j)),
        scratch_shapes=[pltpu.VMEM((tokens, tokens), jnp.bfloat16)],
        compiler_params=pltpu.CompilerParams(vmem_limit_bytes=16 << 20),
        cost_estimate=pl.CostEstimate(
            flops=2 * tokens * derivative.size,
            transcendentals=0,
            bytes_accessed=2 * (late.size + early.size) + 6 * derivative.size,
        ),
    )(target, late, early, pltpu.with_memory_space_constraint(derivative, pltpu.HBM))


def hidden_kernel(rows_ref, weights_ref, out_ref):
    part = weights_ref[...].reshape(-1, weights_ref.shape[-1])
    out_ref[0] = dot(rows_ref[...], part, ((1,), (1,))).astype(out_ref.dtype)


def hidden_terms(rows, weights, first, count):
    tokens, depth = rows.shape
    width = weights.shape[2]
    return pl.pallas_call(
        hidden_kernel,
        grid=(4,),
        out_shape=pltpu.HBM((4, tokens, count * width), jnp.bfloat16),
        in_specs=[
            pl.BlockSpec((tokens, depth), lambda d: (0, 0)),
            pl.BlockSpec((1, count, width, depth), lambda d: (d, first // count, 0, 0)),
        ],
        out_specs=pl.BlockSpec((1, tokens, count * width), lambda d: (d, 0, 0)),
        compiler_params=pltpu.CompilerParams(vmem_limit_bytes=18 << 20),
        cost_estimate=pl.CostEstimate(
            flops=8 * tokens * depth * count * width,
            transcendentals=0,
            bytes_accessed=2 * (tokens * depth + 4 * count * width * (depth + tokens)),
        ),
    )(rows, pltpu.with_memory_space_constraint(weights, pltpu.HBM))


def dot(lhs, rhs, dims):
    return lax.dot_general(lhs, rhs, (dims, ((), ())), preferred_element_type=jnp.float32)


def wide(value):
    return value.astype(jnp.float32)


def narrow(value):
    return value.astype(jnp.bfloat16)


def after(value, *others):
    return lax.optimization_barrier((value, *others))[0]


def gather_ring(value, other):
    half = value.shape[0] // 2
    low, high = value[:half], value[half:]
    first = flip(low, "y", 1), flip(high, "y", 3)
    low, high, one_low, three_high, other = lax.optimization_barrier((low, high, *first, other))
    two_low, two_high = flip(one_low, "y", 3), flip(three_high, "y", 1)
    return [value, one_low, flip(high, "y", 1), flip(low, "y", 3), three_high, two_low, two_high], other


PLANS = (("x", "z", 1), ("z", "x", 1), ("x", "z", 3), ("z", "x", 3))


def arrange_kernel(starts, order_ref, *refs):
    inputs, outputs = refs[: len(starts)], refs[-len(PLANS) :]
    step = pl.program_id(0)
    for k, start in enumerate(starts):
        stop = starts[k + 1] if k + 1 < len(starts) else 16

        @pl.when((step >= start) & (step < stop))
        def _(k=k):
            for out_ref in outputs:
                out_ref[...] = inputs[k][...]


def arrange(pieces, order, offset, before=()):
    starts, total = [], 0
    for piece in pieces:
        starts.append(total)
        total += piece.shape[0]
    block = (1, *pieces[0].shape[1:])

    def source(start, count):
        return lambda i, order: (jnp.clip(i - start, 0, count - 1), 0, 0)

    def target(first, near):
        lead = 3 if near == 1 else 2

        def index(i, order):
            place = lax.shift_right_logical(i + offset, 2)
            z, x = place ^ lax.shift_right_logical(place, 1) ^ order[0], i & 3
            major, minor = (x, z) if first == "x" else (z, x)
            return (((major + lead) & 3) * 4 + minor, 0, 0)

        return index

    size = total * block[1] * block[2] * 2
    return pl.pallas_call(
        functools.partial(arrange_kernel, starts),
        grid_spec=pltpu.PrefetchScalarGridSpec(
            num_scalar_prefetch=1,
            grid=(total,),
            in_specs=[pl.BlockSpec(block, source(s, p.shape[0])) for s, p in zip(starts, pieces)]
            + [pl.BlockSpec(memory_space=pltpu.HBM) for _ in before],
            out_specs=[pl.BlockSpec(block, target(first, near)) for first, _, near in PLANS],
        ),
        out_shape=[pltpu.HBM((16, *block[1:]), jnp.bfloat16) for _ in PLANS],
        input_output_aliases={1 + len(pieces) + i: i for i in range(len(before))},
        compiler_params=pltpu.CompilerParams(vmem_limit_bytes=8 << 20),
        cost_estimate=pl.CostEstimate(flops=0, transcendentals=0, bytes_accessed=5 * size),
    )(order, *pieces, *before)


def product(part, rhs):
    return narrow(dot(part, rhs, ((1,), (0,)))).reshape(2, 4, -1, rhs.shape[1])


SENT = {1: slice(1, 3), 3: slice(2, 4)}
HELD = {1: slice(3, 5), 3: slice(0, 2)}
OWN, FAR = {1: 1, 3: 0}, {1: 0, 3: 1}
OWN_SENT, FAR_SENT = {1: 0, 3: 1}, {1: 1, 3: 0}


def scatter_first(arrived, kept, axis, near):
    far = 4 - near
    arrived_far = flip(narrow(wide(kept[FAR[near]]) + wide(arrived[FAR_SENT[near]])), axis, far)
    return narrow(wide(kept[OWN[near]]) + wide(arrived[OWN_SENT[near]]) + wide(arrived_far))


def scatter_second(total, axis, near):
    far = 4 - near
    arrived = flip(total[SENT[near]], axis, near)
    arrived_far = flip(narrow(wide(total[far]) + wide(arrived[FAR_SENT[near]])), axis, far)
    return wide(total[0]) + wide(arrived[OWN_SENT[near]]) + wide(arrived_far)


def local(grad_rows, img_start, img_len, img_owner, pre_act, w_out):
    stripe, quarter = grad_rows.shape
    owners_total = lax.axis_size(SEQ)
    frames = stripe // FRAME
    here = lax.axis_index(SEQ)
    x, y, z, core = (lax.axis_index(a) for a in ("x", "y", "z", "core"))
    piece = stripe // owners_total

    spread = lax.all_to_all(
        grad_rows.reshape(owners_total, piece, quarter), SEQ, split_axis=0, concat_axis=0, tiled=True
    )

    images = owners_total * frames
    image_ids = jnp.arange(images, dtype=jnp.int32)
    slots = jnp.arange(stripe, dtype=jnp.int32)
    chosen_image = (image_ids % frames == (slots // FRAME)[:, None]) & (img_owner == here)
    packed = (img_start - image_ids * FRAME) * (2 * FRAME) + img_len
    packed = jnp.where(chosen_image, packed, 0).sum(axis=1)
    offset, length = packed // (2 * FRAME), packed % (2 * FRAME)
    target = jnp.where(slots % FRAME < length, slots + offset, -1)
    chosen = (target[:, None] == slots).astype(jnp.bfloat16)

    units = pre_act.shape[1]
    _, derivative = gelu_parts(dot(chosen, pre_act, ((0,), (0,))))
    activation, _ = gelu_parts(dot(pre_act, chosen, ((0,), (0,))))
    halves = narrow(activation).reshape(4, 2, units // 8, stripe)

    def half_of(which):
        shape = (1, 1, *halves.shape[2:])
        parts = [lax.dynamic_slice(halves, (x ^ m, which, 0, 0), shape)[:, 0] for m in range(4)]
        return jnp.concatenate(parts, axis=0)

    both = jnp.concatenate([half_of(core), flip(half_of(1 - core), "core", 1)], axis=2)
    pieces, spread = gather_ring(both, spread)
    order = (y ^ z).reshape(1)
    arranged = arrange(pieces[5:], order, 12, arrange(pieces[:5], order, 0))
    owners = img_owner.reshape(owners_total, frames)
    frame_here = here * piece // FRAME
    owner_here = lax.dynamic_index_in_dim(owners, frame_here, 1, keepdims=False)
    placed = place(owner_here, spread)
    rows = lax.all_to_all(placed, SEQ, split_axis=0, concat_axis=0, tiled=True).reshape(stripe, quarter)
    lhs = [part.reshape(-1, 2 * stripe) for part in arranged]
    weights = w_out.reshape(4, 5, units // 5, quarter)
    rows, weights, lhs, derivative = lax.optimization_barrier((rows, weights, lhs, derivative))

    def exchange(terms):
        return lax.all_to_all(terms, "y", split_axis=0, concat_axis=0, tiled=True)

    early = hidden_terms(rows, weights, 4, 1)

    pair = jnp.concatenate([rows, flip(rows, "core", 1)], axis=0)
    span = quarter // 4
    columns = [pair[:, i * span : (i + 1) * span] for i in range(4)]
    terms = [product(part[: part.shape[0] // 2], c) for part, c in zip(lhs, columns)]
    landed = [flip(term, first, near) for (first, _, near), term in zip(PLANS, terms)]

    done = [term[0, 0, :8, :128] for term in terms]
    early = exchange(after(early, *done))
    late = hidden_terms(rows, after(weights, *done), 0, 4)
    lhs, early, _ = lax.optimization_barrier((lhs, early, late))
    late = exchange(late)
    kept = [product(part[part.shape[0] // 2 :], c) for part, c in zip(lhs, columns)]

    totals = [scatter_first(a, k, first, near) for a, k, (first, _, near) in zip(landed, kept, PLANS)]
    sums = [scatter_second(t, second, near) for t, (_, second, near) in zip(totals, PLANS)]
    factor = 1.0 / math.sqrt(owners_total * stripe)
    weight_grad = narrow(jnp.concatenate(sums, axis=1) * factor)
    pre_grad = finish(target[:, None], late, early, derivative)
    return (pre_grad, weight_grad)


def solution(mesh):
    grid = Mesh(mesh.devices.reshape(4, 4, 2, 4), ("z", "x", "core", "y"))
    return jax.shard_map(
        local,
        mesh=grid,
        in_specs=(P(SEQ, "y"), P(), P(), P(), P(SEQ, "y"), P(None, "y")),
        out_specs=(P(SEQ, "y"), P(SEQ, "y")),
        check_vma=False,
    )
```

```python
import functools
import math

import jax
import jax.numpy as jnp
from jax import lax
from jax.experimental import pallas as pl
from jax.experimental.pallas import tpu as pltpu
from jax.sharding import Mesh
from jax.sharding import PartitionSpec as P

FRAME = 64
SEQ = ("z", "x", "core")


def flip(value, axis, mask):
    size = lax.axis_size(axis)
    return lax.ppermute(value, axis, [(i, i ^ mask) for i in range(size)])


def gelu_parts(values):
    normal_cdf = 0.5 * (1.0 + lax.erf(values * 0.7071067811865476))
    density = jnp.exp(-0.5 * values * values) * 0.3989422804014327
    return (values * normal_cdf, normal_cdf + values * density)


def place_kernel(owner_ref, blocks_ref, out_ref, staged, in_sems, out_sems):
    count = blocks_ref.shape[0]

    def read(i):
        return pltpu.make_async_copy(blocks_ref.at[i], staged.at[i], in_sems.at[i])

    def write(i):
        return pltpu.make_async_copy(staged.at[i], out_ref.at[owner_ref[i]], out_sems.at[i])

    def start(i, carry):
        read(i).start()
        return carry

    def move(i, carry):
        read(i).wait()
        write(i).start()
        return carry

    def wait(i, carry):
        write(i).wait()
        return carry

    for step in (start, move, wait):
        lax.fori_loop(0, count, step, 0)


def place(owner, blocks):
    return pl.pallas_call(
        place_kernel,
        out_shape=pltpu.HBM(blocks.shape, blocks.dtype),
        in_specs=[pl.BlockSpec(memory_space=pltpu.SMEM), pl.BlockSpec(memory_space=pltpu.HBM)],
        out_specs=pl.BlockSpec(memory_space=pltpu.HBM),
        scratch_shapes=[
            pltpu.VMEM(blocks.shape, blocks.dtype),
            pltpu.SemaphoreType.DMA((blocks.shape[0],)),
            pltpu.SemaphoreType.DMA((blocks.shape[0],)),
        ],
        compiler_params=pltpu.CompilerParams(vmem_limit_bytes=8 << 20),
        cost_estimate=pl.CostEstimate(
            flops=0, transcendentals=0, bytes_accessed=2 * blocks.size * blocks.dtype.itemsize
        ),
    )(owner, blocks)


def finish_kernel(target_ref, late_ref, early_ref, derivative_ref, out_ref):
    count = target_ref.shape[0]
    rows = lax.broadcasted_iota(jnp.int32, (count, count), 1) + pl.program_id(0) * count
    chosen = jnp.where(rows == target_ref[...], 1.0, 0.0).astype(jnp.bfloat16)
    start = 0
    for ref in (late_ref, early_ref):
        stop = start + ref.shape[2]
        total = wide(ref[0]) + wide(ref[1]) + wide(ref[2]) + wide(ref[3])
        grad = narrow(total * derivative_ref[:, start:stop])
        out_ref[:, start:stop] = narrow(dot(chosen, grad, ((1,), (0,))))
        start = stop


def finish(target, late, early, derivative):
    tokens, units = derivative.shape
    rows = 2 * FRAME

    def arrived(part):
        return pl.BlockSpec((4, rows, part.shape[2]), lambda i: (0, i, 0))

    return pl.pallas_call(
        finish_kernel,
        grid=(tokens // rows,),
        out_shape=jax.ShapeDtypeStruct(derivative.shape, jnp.bfloat16),
        in_specs=[
            pl.BlockSpec((rows, 1), lambda i: (i, 0)),
            arrived(late),
            arrived(early),
            pl.BlockSpec((rows, units), lambda i: (i, 0)),
        ],
        out_specs=pl.BlockSpec((rows, units), lambda i: (i, 0)),
        compiler_params=pltpu.CompilerParams(vmem_limit_bytes=16 << 20),
        cost_estimate=pl.CostEstimate(
            flops=2 * tokens * derivative.size,
            transcendentals=0,
            bytes_accessed=2 * (late.size + early.size) + 6 * derivative.size,
        ),
    )(target, late, early, pltpu.with_memory_space_constraint(derivative, pltpu.HBM))


def hidden_kernel(rows_ref, weights_ref, out_ref):
    part = weights_ref[...].reshape(-1, weights_ref.shape[-1])
    out_ref[0] = dot(rows_ref[...], part, ((1,), (1,))).astype(out_ref.dtype)


def hidden_terms(rows, weights, first, count):
    tokens, depth = rows.shape
    width = weights.shape[2]
    return pl.pallas_call(
        hidden_kernel,
        grid=(4,),
        out_shape=pltpu.HBM((4, tokens, count * width), jnp.bfloat16),
        in_specs=[
            pl.BlockSpec((tokens, depth), lambda d: (0, 0)),
            pl.BlockSpec((1, count, width, depth), lambda d: (d, first // count, 0, 0)),
        ],
        out_specs=pl.BlockSpec((1, tokens, count * width), lambda d: (d, 0, 0)),
        compiler_params=pltpu.CompilerParams(vmem_limit_bytes=18 << 20),
        cost_estimate=pl.CostEstimate(
            flops=8 * tokens * depth * count * width,
            transcendentals=0,
            bytes_accessed=2 * (tokens * depth + 4 * count * width * (depth + tokens)),
        ),
    )(rows, pltpu.with_memory_space_constraint(weights, pltpu.HBM))


def dot(lhs, rhs, dims):
    return lax.dot_general(lhs, rhs, (dims, ((), ())), preferred_element_type=jnp.float32)


def wide(value):
    return value.astype(jnp.float32)


def narrow(value):
    return value.astype(jnp.bfloat16)


def after(value, *others):
    return lax.optimization_barrier((value, *others))[0]


def gather_ring(value, other):
    half = value.shape[0] // 2
    low, high = value[:half], value[half:]
    first = flip(low, "y", 1), flip(high, "y", 3)
    low, high, one_low, three_high, other = lax.optimization_barrier((low, high, *first, other))
    two_low, two_high = flip(one_low, "y", 3), flip(three_high, "y", 1)
    return [value, one_low, flip(high, "y", 1), flip(low, "y", 3), three_high, two_low, two_high], other


PLANS = (("x", "z", 1), ("z", "x", 1), ("x", "z", 3), ("z", "x", 3))


def arrange_kernel(starts, order_ref, *refs):
    inputs, outputs = refs[: len(starts)], refs[-len(PLANS) :]
    step = pl.program_id(0)
    for k, start in enumerate(starts):
        stop = starts[k + 1] if k + 1 < len(starts) else 16

        @pl.when((step >= start) & (step < stop))
        def _(k=k):
            for out_ref in outputs:
                out_ref[...] = inputs[k][...]


def arrange(pieces, order, offset, before=()):
    starts, total = [], 0
    for piece in pieces:
        starts.append(total)
        total += piece.shape[0]
    block = (1, *pieces[0].shape[1:])

    def source(start, count):
        return lambda i, order: (jnp.clip(i - start, 0, count - 1), 0, 0)

    def target(first, near):
        lead = 3 if near == 1 else 2

        def index(i, order):
            place = lax.shift_right_logical(i + offset, 2)
            z, x = place ^ lax.shift_right_logical(place, 1) ^ order[0], i & 3
            major, minor = (x, z) if first == "x" else (z, x)
            return (((major + lead) & 3) * 4 + minor, 0, 0)

        return index

    size = total * block[1] * block[2] * 2
    return pl.pallas_call(
        functools.partial(arrange_kernel, starts),
        grid_spec=pltpu.PrefetchScalarGridSpec(
            num_scalar_prefetch=1,
            grid=(total,),
            in_specs=[pl.BlockSpec(block, source(s, p.shape[0])) for s, p in zip(starts, pieces)]
            + [pl.BlockSpec(memory_space=pltpu.HBM) for _ in before],
            out_specs=[pl.BlockSpec(block, target(first, near)) for first, _, near in PLANS],
        ),
        out_shape=[pltpu.HBM((16, *block[1:]), jnp.bfloat16) for _ in PLANS],
        input_output_aliases={1 + len(pieces) + i: i for i in range(len(before))},
        compiler_params=pltpu.CompilerParams(vmem_limit_bytes=8 << 20),
        cost_estimate=pl.CostEstimate(flops=0, transcendentals=0, bytes_accessed=5 * size),
    )(order, *pieces, *before)


def product(part, rhs):
    return narrow(dot(part, rhs, ((1,), (0,)))).reshape(2, 4, -1, rhs.shape[1])


SENT = {1: slice(1, 3), 3: slice(2, 4)}
HELD = {1: slice(3, 5), 3: slice(0, 2)}
OWN, FAR = {1: 1, 3: 0}, {1: 0, 3: 1}
OWN_SENT, FAR_SENT = {1: 0, 3: 1}, {1: 1, 3: 0}


def scatter_first(arrived, kept, axis, near):
    far = 4 - near
    arrived_far = flip(narrow(wide(kept[FAR[near]]) + wide(arrived[FAR_SENT[near]])), axis, far)
    return narrow(wide(kept[OWN[near]]) + wide(arrived[OWN_SENT[near]]) + wide(arrived_far))


def scatter_second(total, axis, near):
    far = 4 - near
    arrived = flip(total[SENT[near]], axis, near)
    arrived_far = flip(narrow(wide(total[far]) + wide(arrived[FAR_SENT[near]])), axis, far)
    return wide(total[0]) + wide(arrived[OWN_SENT[near]]) + wide(arrived_far)


def local(grad_rows, img_start, img_len, img_owner, pre_act, w_out):
    stripe, quarter = grad_rows.shape
    owners_total = lax.axis_size(SEQ)
    frames = stripe // FRAME
    here = lax.axis_index(SEQ)
    x, y, z, core = (lax.axis_index(a) for a in ("x", "y", "z", "core"))
    piece = stripe // owners_total

    spread = lax.all_to_all(
        grad_rows.reshape(owners_total, piece, quarter), SEQ, split_axis=0, concat_axis=0, tiled=True
    )

    images = owners_total * frames
    image_ids = jnp.arange(images, dtype=jnp.int32)
    slots = jnp.arange(stripe, dtype=jnp.int32)
    chosen_image = (image_ids % frames == (slots // FRAME)[:, None]) & (img_owner == here)
    packed = (img_start - image_ids * FRAME) * (2 * FRAME) + img_len
    packed = jnp.where(chosen_image, packed, 0).sum(axis=1)
    offset, length = packed // (2 * FRAME), packed % (2 * FRAME)
    target = jnp.where(slots % FRAME < length, slots + offset, -1)
    chosen = (target[:, None] == slots).astype(jnp.bfloat16)

    units = pre_act.shape[1]
    _, derivative = gelu_parts(dot(chosen, pre_act, ((0,), (0,))))
    activation, _ = gelu_parts(dot(pre_act, chosen, ((0,), (0,))))
    halves = narrow(activation).reshape(4, 2, units // 8, stripe)

    def half_of(which):
        shape = (1, 1, *halves.shape[2:])
        parts = [lax.dynamic_slice(halves, (x ^ m, which, 0, 0), shape)[:, 0] for m in range(4)]
        return jnp.concatenate(parts, axis=0)

    both = jnp.concatenate([half_of(core), flip(half_of(1 - core), "core", 1)], axis=2)
    pieces, spread = gather_ring(both, spread)
    order = (y ^ z).reshape(1)
    arranged = arrange(pieces[5:], order, 12, arrange(pieces[:5], order, 0))
    owners = img_owner.reshape(owners_total, frames)
    frame_here = here * piece // FRAME
    owner_here = lax.dynamic_index_in_dim(owners, frame_here, 1, keepdims=False)
    placed = place(owner_here, spread)
    rows = lax.all_to_all(placed, SEQ, split_axis=0, concat_axis=0, tiled=True).reshape(stripe, quarter)
    lhs = [part.reshape(-1, 2 * stripe) for part in arranged]
    weights = w_out.reshape(4, 5, units // 5, quarter)
    rows, weights, lhs, derivative = lax.optimization_barrier((rows, weights, lhs, derivative))

    def exchange(terms):
        return lax.all_to_all(terms, "y", split_axis=0, concat_axis=0, tiled=True)

    early = hidden_terms(rows, weights, 4, 1)

    pair = jnp.concatenate([rows, flip(rows, "core", 1)], axis=0)
    span = quarter // 4
    columns = [pair[:, i * span : (i + 1) * span] for i in range(4)]
    terms = [product(part[: part.shape[0] // 2], c) for part, c in zip(lhs, columns)]
    landed = [flip(term, first, near) for (first, _, near), term in zip(PLANS, terms)]

    done = [term[0, 0, :8, :128] for term in terms]
    early = exchange(after(early, *done))
    late = hidden_terms(rows, after(weights, *done), 0, 4)
    lhs, early, _ = lax.optimization_barrier((lhs, early, late))
    late = exchange(late)
    kept = [product(part[part.shape[0] // 2 :], c) for part, c in zip(lhs, columns)]

    totals = [scatter_first(a, k, first, near) for a, k, (first, _, near) in zip(landed, kept, PLANS)]
    sums = [scatter_second(t, second, near) for t, (_, second, near) in zip(totals, PLANS)]
    factor = 1.0 / math.sqrt(owners_total * stripe)
    weight_grad = narrow(jnp.concatenate(sums, axis=1) * factor)
    pre_grad = finish(target[:, None], late, early, derivative)
    return (pre_grad, weight_grad)


def solution(mesh):
    grid = Mesh(mesh.devices.reshape(4, 4, 2, 4), ("z", "x", "core", "y"))
    return jax.shard_map(
        local,
        mesh=grid,
        in_specs=(P(SEQ, "y"), P(), P(), P(), P(SEQ, "y"), P(None, "y")),
        out_specs=(P(SEQ, "y"), P(SEQ, "y")),
        check_vma=False,
    )
```

```python
import functools
import math

import jax
import jax.numpy as jnp
from jax import lax
from jax.experimental import pallas as pl
from jax.experimental.pallas import tpu as pltpu
from jax.sharding import Mesh
from jax.sharding import PartitionSpec as P

FRAME = 64
SEQ = ("z", "x", "core")


def flip(value, axis, mask):
    size = lax.axis_size(axis)
    return lax.ppermute(value, axis, [(i, i ^ mask) for i in range(size)])


def gelu_parts(values):
    normal_cdf = 0.5 * (1.0 + lax.erf(values * 0.7071067811865476))
    density = jnp.exp(-0.5 * values * values) * 0.3989422804014327
    return (values * normal_cdf, normal_cdf + values * density)


def place_kernel(owner_ref, blocks_ref, out_ref, staged, in_sems, out_sems):
    count = blocks_ref.shape[0]

    def read(i):
        return pltpu.make_async_copy(blocks_ref.at[i], staged.at[i], in_sems.at[i])

    def write(i):
        return pltpu.make_async_copy(staged.at[i], out_ref.at[owner_ref[i]], out_sems.at[i])

    def start(i, carry):
        read(i).start()
        return carry

    def move(i, carry):
        read(i).wait()
        write(i).start()
        return carry

    def wait(i, carry):
        write(i).wait()
        return carry

    for step in (start, move, wait):
        lax.fori_loop(0, count, step, 0)


def place(owner, blocks):
    return pl.pallas_call(
        place_kernel,
        out_shape=pltpu.HBM(blocks.shape, blocks.dtype),
        in_specs=[pl.BlockSpec(memory_space=pltpu.SMEM), pl.BlockSpec(memory_space=pltpu.HBM)],
        out_specs=pl.BlockSpec(memory_space=pltpu.HBM),
        scratch_shapes=[
            pltpu.VMEM(blocks.shape, blocks.dtype),
            pltpu.SemaphoreType.DMA((blocks.shape[0],)),
            pltpu.SemaphoreType.DMA((blocks.shape[0],)),
        ],
        compiler_params=pltpu.CompilerParams(vmem_limit_bytes=8 << 20),
        cost_estimate=pl.CostEstimate(
            flops=0, transcendentals=0, bytes_accessed=2 * blocks.size * blocks.dtype.itemsize
        ),
    )(owner, blocks)


def finish_kernel(target_ref, late_ref, early_ref, derivative_ref, out_ref):
    count = target_ref.shape[0]
    rows = lax.broadcasted_iota(jnp.int32, (count, count), 1) + pl.program_id(0) * count
    chosen = jnp.where(rows == target_ref[...], 1.0, 0.0).astype(jnp.bfloat16)
    start = 0
    for ref in (late_ref, early_ref):
        stop = start + ref.shape[2]
        total = wide(ref[0]) + wide(ref[1]) + wide(ref[2]) + wide(ref[3])
        grad = narrow(total * derivative_ref[:, start:stop])
        out_ref[:, start:stop] = narrow(dot(chosen, grad, ((1,), (0,))))
        start = stop


def finish(target, late, early, derivative):
    tokens, units = derivative.shape
    rows = FRAME

    def arrived(part):
        return pl.BlockSpec((4, rows, part.shape[2]), lambda i: (0, i, 0))

    return pl.pallas_call(
        finish_kernel,
        grid=(tokens // rows,),
        out_shape=jax.ShapeDtypeStruct(derivative.shape, jnp.bfloat16),
        in_specs=[
            pl.BlockSpec((rows, 1), lambda i: (i, 0)),
            arrived(late),
            arrived(early),
            pl.BlockSpec((rows, units), lambda i: (i, 0)),
        ],
        out_specs=pl.BlockSpec((rows, units), lambda i: (i, 0)),
        compiler_params=pltpu.CompilerParams(vmem_limit_bytes=16 << 20),
        cost_estimate=pl.CostEstimate(
            flops=2 * tokens * derivative.size,
            transcendentals=0,
            bytes_accessed=2 * (late.size + early.size) + 6 * derivative.size,
        ),
    )(target, late, early, pltpu.with_memory_space_constraint(derivative, pltpu.HBM))


def hidden_kernel(rows_ref, weights_ref, out_ref):
    part = weights_ref[...].reshape(-1, weights_ref.shape[-1])
    out_ref[0] = dot(rows_ref[...], part, ((1,), (1,))).astype(out_ref.dtype)


def hidden_terms(rows, weights, first, count):
    tokens, depth = rows.shape
    width = weights.shape[2]
    return pl.pallas_call(
        hidden_kernel,
        grid=(4,),
        out_shape=pltpu.HBM((4, tokens, count * width), jnp.bfloat16),
        in_specs=[
            pl.BlockSpec((tokens, depth), lambda d: (0, 0)),
            pl.BlockSpec((1, count, width, depth), lambda d: (d, first // count, 0, 0)),
        ],
        out_specs=pl.BlockSpec((1, tokens, count * width), lambda d: (d, 0, 0)),
        compiler_params=pltpu.CompilerParams(vmem_limit_bytes=18 << 20),
        cost_estimate=pl.CostEstimate(
            flops=8 * tokens * depth * count * width,
            transcendentals=0,
            bytes_accessed=2 * (tokens * depth + 4 * count * width * (depth + tokens)),
        ),
    )(rows, pltpu.with_memory_space_constraint(weights, pltpu.HBM))


def dot(lhs, rhs, dims):
    return lax.dot_general(lhs, rhs, (dims, ((), ())), preferred_element_type=jnp.float32)


def wide(value):
    return value.astype(jnp.float32)


def narrow(value):
    return value.astype(jnp.bfloat16)


def after(value, *others):
    return lax.optimization_barrier((value, *others))[0]


def gather_ring(value, other):
    half = value.shape[0] // 2
    low, high = value[:half], value[half:]
    first = flip(low, "y", 1), flip(high, "y", 3)
    low, high, one_low, three_high, other = lax.optimization_barrier((low, high, *first, other))
    two_low, two_high = flip(one_low, "y", 3), flip(three_high, "y", 1)
    return [value, one_low, flip(high, "y", 1), flip(low, "y", 3), three_high, two_low, two_high], other


PLANS = (("x", "z", 1), ("z", "x", 1), ("x", "z", 3), ("z", "x", 3))


def arrange_kernel(starts, order_ref, *refs):
    inputs, outputs = refs[: len(starts)], refs[-len(PLANS) :]
    step = pl.program_id(0)
    for k, start in enumerate(starts):
        stop = starts[k + 1] if k + 1 < len(starts) else 16

        @pl.when((step >= start) & (step < stop))
        def _(k=k):
            for out_ref in outputs:
                out_ref[...] = inputs[k][...]


def arrange(pieces, order, offset, before=()):
    starts, total = [], 0
    for piece in pieces:
        starts.append(total)
        total += piece.shape[0]
    block = (1, *pieces[0].shape[1:])

    def source(start, count):
        return lambda i, order: (jnp.clip(i - start, 0, count - 1), 0, 0)

    def target(first, near):
        lead = 3 if near == 1 else 2

        def index(i, order):
            place = lax.shift_right_logical(i + offset, 2)
            z, x = place ^ lax.shift_right_logical(place, 1) ^ order[0], i & 3
            major, minor = (x, z) if first == "x" else (z, x)
            return (((major + lead) & 3) * 4 + minor, 0, 0)

        return index

    size = total * block[1] * block[2] * 2
    return pl.pallas_call(
        functools.partial(arrange_kernel, starts),
        grid_spec=pltpu.PrefetchScalarGridSpec(
            num_scalar_prefetch=1,
            grid=(total,),
            in_specs=[pl.BlockSpec(block, source(s, p.shape[0])) for s, p in zip(starts, pieces)]
            + [pl.BlockSpec(memory_space=pltpu.HBM) for _ in before],
            out_specs=[pl.BlockSpec(block, target(first, near)) for first, _, near in PLANS],
        ),
        out_shape=[pltpu.HBM((16, *block[1:]), jnp.bfloat16) for _ in PLANS],
        input_output_aliases={1 + len(pieces) + i: i for i in range(len(before))},
        compiler_params=pltpu.CompilerParams(vmem_limit_bytes=8 << 20),
        cost_estimate=pl.CostEstimate(flops=0, transcendentals=0, bytes_accessed=5 * size),
    )(order, *pieces, *before)


def product(part, rhs):
    return narrow(dot(part, rhs, ((1,), (0,)))).reshape(2, 4, -1, rhs.shape[1])


SENT = {1: slice(1, 3), 3: slice(2, 4)}
HELD = {1: slice(3, 5), 3: slice(0, 2)}
OWN, FAR = {1: 1, 3: 0}, {1: 0, 3: 1}
OWN_SENT, FAR_SENT = {1: 0, 3: 1}, {1: 1, 3: 0}


def scatter_first(arrived, kept, axis, near):
    far = 4 - near
    arrived_far = flip(narrow(wide(kept[FAR[near]]) + wide(arrived[FAR_SENT[near]])), axis, far)
    return narrow(wide(kept[OWN[near]]) + wide(arrived[OWN_SENT[near]]) + wide(arrived_far))


def scatter_second(total, axis, near):
    far = 4 - near
    arrived = flip(total[SENT[near]], axis, near)
    arrived_far = flip(narrow(wide(total[far]) + wide(arrived[FAR_SENT[near]])), axis, far)
    return wide(total[0]) + wide(arrived[OWN_SENT[near]]) + wide(arrived_far)


def local(grad_rows, img_start, img_len, img_owner, pre_act, w_out):
    stripe, quarter = grad_rows.shape
    owners_total = lax.axis_size(SEQ)
    frames = stripe // FRAME
    here = lax.axis_index(SEQ)
    x, y, z, core = (lax.axis_index(a) for a in ("x", "y", "z", "core"))
    piece = stripe // owners_total

    spread = lax.all_to_all(
        grad_rows.reshape(owners_total, piece, quarter), SEQ, split_axis=0, concat_axis=0, tiled=True
    )

    images = owners_total * frames
    image_ids = jnp.arange(images, dtype=jnp.int32)
    slots = jnp.arange(stripe, dtype=jnp.int32)
    chosen_image = (image_ids % frames == (slots // FRAME)[:, None]) & (img_owner == here)
    packed = (img_start - image_ids * FRAME) * (2 * FRAME) + img_len
    packed = jnp.where(chosen_image, packed, 0).sum(axis=1)
    offset, length = packed // (2 * FRAME), packed % (2 * FRAME)
    target = jnp.where(slots % FRAME < length, slots + offset, -1)
    chosen = (target[:, None] == slots).astype(jnp.bfloat16)

    units = pre_act.shape[1]
    _, derivative = gelu_parts(dot(chosen, pre_act, ((0,), (0,))))
    activation, _ = gelu_parts(dot(pre_act, chosen, ((0,), (0,))))
    halves = narrow(activation).reshape(4, 2, units // 8, stripe)

    def half_of(which):
        shape = (1, 1, *halves.shape[2:])
        parts = [lax.dynamic_slice(halves, (x ^ m, which, 0, 0), shape)[:, 0] for m in range(4)]
        return jnp.concatenate(parts, axis=0)

    both = jnp.concatenate([half_of(core), flip(half_of(1 - core), "core", 1)], axis=2)
    pieces, spread = gather_ring(both, spread)
    order = (y ^ z).reshape(1)
    arranged = arrange(pieces[5:], order, 12, arrange(pieces[:5], order, 0))
    owners = img_owner.reshape(owners_total, frames)
    frame_here = here * piece // FRAME
    owner_here = lax.dynamic_index_in_dim(owners, frame_here, 1, keepdims=False)
    placed = place(owner_here, spread)
    rows = lax.all_to_all(placed, SEQ, split_axis=0, concat_axis=0, tiled=True).reshape(stripe, quarter)
    lhs = [part.reshape(-1, 2 * stripe) for part in arranged]
    weights = w_out.reshape(4, 5, units // 5, quarter)
    rows, weights, lhs, derivative = lax.optimization_barrier((rows, weights, lhs, derivative))

    def exchange(terms):
        return lax.all_to_all(terms, "y", split_axis=0, concat_axis=0, tiled=True)

    early = hidden_terms(rows, weights, 4, 1)

    pair = jnp.concatenate([rows, flip(rows, "core", 1)], axis=0)
    span = quarter // 4
    columns = [pair[:, i * span : (i + 1) * span] for i in range(4)]
    terms = [product(part[: part.shape[0] // 2], c) for part, c in zip(lhs, columns)]
    landed = [flip(term, first, near) for (first, _, near), term in zip(PLANS, terms)]

    done = [term[0, 0, :8, :128] for term in terms]
    early = exchange(after(early, *done))
    late = hidden_terms(rows, after(weights, *done), 0, 4)
    lhs, early, _ = lax.optimization_barrier((lhs, early, late))
    late = exchange(late)
    kept = [product(part[part.shape[0] // 2 :], c) for part, c in zip(lhs, columns)]

    totals = [scatter_first(a, k, first, near) for a, k, (first, _, near) in zip(landed, kept, PLANS)]
    sums = [scatter_second(t, second, near) for t, (_, second, near) in zip(totals, PLANS)]
    factor = 1.0 / math.sqrt(owners_total * stripe)
    weight_grad = narrow(jnp.concatenate(sums, axis=1) * factor)
    pre_grad = finish(target[:, None], late, early, derivative)
    return (pre_grad, weight_grad)


def solution(mesh):
    grid = Mesh(mesh.devices.reshape(4, 4, 2, 4), ("z", "x", "core", "y"))
    return jax.shard_map(
        local,
        mesh=grid,
        in_specs=(P(SEQ, "y"), P(), P(), P(), P(SEQ, "y"), P(None, "y")),
        out_specs=(P(SEQ, "y"), P(SEQ, "y")),
        check_vma=False,
    )
```
